32 devices in a mesh: dp: 4 (over z), blk: 4 (over x, core), seq: 2 (over y).
Axes of the slice: x: 2, y: 2, z: 4, core: 2. Of those that a mesh axis runs over, the one named last changes fastest.
Arguments:
- inputs: bfloat16 [4096, 2304], P(('dp', 'blk', 'seq')), may hold values from -6 to 6
- teacher: bfloat16 [4096, 2304], P(('dp', 'blk', 'seq')), may hold values from -6 to 6
- valid_mask: int32 [4096], replicated, may hold values 0 or 1
- doc_lengths: int32 [4, 8], replicated, may hold values from 1 to 512, 1024 in all within a row
- gain_pre_attention: bfloat16 [2304], P(('dp', 'blk', 'seq')), may hold values from 0.099609375 to 1.8984375
- query_weight: bfloat16 [2304, 2048], P(('dp', 'blk'), 'seq'), may hold values from -0.125 to 0.125
- key_weight: bfloat16 [2304, 1024], P(('dp', 'blk', 'seq')), may hold values from -0.125 to 0.125
- value_weight: bfloat16 [2304, 1024], P(('dp', 'blk', 'seq')), may hold values from -0.125 to 0.125
- output_weight: bfloat16 [2048, 2304], P('seq', ('dp', 'blk')), may hold values from -0.125 to 0.125
- gain_post_attention: bfloat16 [2304], P(('dp', 'blk', 'seq')), may hold values from 0.099609375 to 1.8984375
- gain_pre_feed: bfloat16 [2304], P(('dp', 'blk', 'seq')), may hold values from 0.099609375 to 1.8984375
- gate_weight: bfloat16 [2304, 9216], P(('dp', 'blk'), 'seq'), may hold values from -0.125 to 0.125
- up_weight: bfloat16 [2304, 9216], P(('dp', 'blk'), 'seq'), may hold values from -0.125 to 0.125
- down_weight: bfloat16 [9216, 2304], P('seq', ('dp', 'blk')), may hold values from -0.0625 to 0.0625
- gain_post_feed: bfloat16 [2304], P(('dp', 'blk', 'seq')), may hold values from 0.099609375 to 1.8984375
Outputs:
- layer_output: bfloat16 [4096, 2304], P(('dp', 'blk', 'seq'))
- teacher_loss: float32 [], replicated
- inputs_gradient: float32 [4096, 2304], P(('dp', 'blk', 'seq'))
- gain_pre_attention_gradient: float32 [2304], P(('dp', 'blk', 'seq'))
- query_weight_gradient: float32 [2304, 2048], P(('dp', 'blk'), 'seq')
- key_weight_gradient: float32 [2304, 1024], P(('dp', 'blk', 'seq'))
- value_weight_gradient: float32 [2304, 1024], P(('dp', 'blk', 'seq'))
- output_weight_gradient: float32 [2048, 2304], P('seq', ('dp', 'blk'))
- gain_post_attention_gradient: float32 [2304], P(('dp', 'blk', 'seq'))
- gain_pre_feed_gradient: float32 [2304], P(('dp', 'blk', 'seq'))
- gate_weight_gradient: float32 [2304, 9216], P(('dp', 'blk'), 'seq')
- up_weight_gradient: float32 [2304, 9216], P(('dp', 'blk'), 'seq')
- down_weight_gradient: float32 [9216, 2304], P('seq', ('dp', 'blk'))
- gain_post_feed_gradient: float32 [2304], P(('dp', 'blk', 'seq'))
The draws below stay inside these ranges and needn't reach their ends.
Inputs may be any that keep to these rules, and one draw needn't show every extreme that they name: `doc_lengths`: each row fills one sequence of 1024 tokens; its last span is padding; the largest entry of each row is exactly 512.
All inputs are finite; a program needn't handle non-finite values.
Results may differ from the reference program's by a relative error of at most 0.02.
Values may be sent and summed in bfloat16 or wider, within the bound.
A program may use at most 320 MiB of HBM per device.

```python
import math
import jax
import jax.numpy as jnp
import numpy as np
from jax import lax

D = 2304
FF = 9216
HQ = 8
KVH = 4
HD = 256
NDOC = 8
SEQ_LEN = 1024
SEQS = 4
TOKENS = 4096
DOC_MOST = 512
N_SEQ = 2


def with_ends(array, key, low, largest):
    dims = array.shape
    index_at = [jax.random.randint(jax.random.fold_in(key, axis), (), 0, dims[axis]) for axis in range(len(dims))]
    array = array.at[tuple(index_at)].set(low)
    longest = dims.index(max(dims))
    index_at[longest] = (index_at[longest] + 1) % dims[longest]
    return array.at[tuple(index_at)].set(largest)


def spiked(drawn, key, source, target, parts, factor):
    def block_of(axis_at):
        return (jnp.arange(drawn.shape[axis_at]) // (drawn.shape[axis_at] // parts)).reshape((-1,) + (1,) * (drawn.ndim - 1 - axis_at))

    one_side = jax.random.permutation(key, parts)[block_of(target)]
    far = (block_of(target) + parts // 2) % parts
    return jnp.where((block_of(source) == one_side) | (block_of(source) == far), factor * drawn, drawn)


def shard_levels(own_key, shape, shards, low, high):
    level = 1.0
    for dim, blocks in shards:
        steps = jax.random.uniform(jax.random.fold_in(jax.random.fold_in(own_key, 6), dim), (blocks,), jnp.float32, low / len(shards), high / len(shards))
        level = level * jnp.repeat(jnp.exp(steps), shape[dim] // blocks).reshape((-1,) + (1,) * (len(shape) - 1 - dim))
    return level


def split_up(count, total, reach, slope):
    portions = [(1 << 20) // math.isqrt(standing ** slope) + 1 for standing in range(2, count + 1)]
    surplus, given = total - reach - (count - 1), [1] * (count - 1)
    while surplus > 0:
        movable = [i for i in range(count - 1) if given[i] < reach]
        whole, left = sum([portions[i] for i in movable]), surplus
        for i in movable:
            more = min(reach - given[i], max(1, left * portions[i] // whole), surplus)
            given[i] = given[i] + more
            surplus = surplus - more
    return np.array([reach] + given)


def ragged_sizes(rng, number_of, total, bound, slope):
    if number_of == 2:
        one = jax.random.randint(rng, (), max(1, total - bound), min(bound, total - 1) + 1)
        return jnp.stack([one, total - one])
    sizes = jnp.asarray(split_up(number_of, total, bound, slope), jnp.int32)
    pairs = (number_of - 1) // 2
    donor, sink = sizes[1:1 + 2 * pairs:2], sizes[2:2 + 2 * pairs:2]
    slack = jnp.minimum(donor - 1, bound - sink)
    passed = jax.random.randint(jax.random.fold_in(rng, 1), (pairs,), 0, 1 << 20) % (slack + 1)
    sizes = sizes.at[1:1 + 2 * pairs:2].set(donor - passed).at[2:2 + 2 * pairs:2].set(sink + passed)
    return sizes[jax.random.permutation(jax.random.fold_in(rng, 2), number_of)]


def noise(own_key, dims, deviation, most, cuts=(), kind=jnp.bfloat16):
    values = jax.random.normal(own_key, dims, jnp.float32) * deviation
    if len(cuts) > 0:
        values = shard_levels(own_key, dims, cuts, -0.22, 0.18) * values
    return jnp.clip(values, min=-most, max=most).astype(kind)


def heavy_noise(own_key, extent, scale, limit, split, heavy, held_as=jnp.bfloat16):
    result = scale * jax.random.normal(own_key, extent, jnp.float32)
    if split:
        result = result * shard_levels(own_key, extent, split, -0.22, 0.18)
    return jnp.clip(spiked(result, jax.random.fold_in(own_key, 3), *heavy), -limit, limit).astype(held_as)


def setup_inputs(seed: int = 0) -> dict:
    streams_of = jax.random.split(jax.random.key(seed), 16)
    inputs = heavy_noise(streams_of[0], (TOKENS, D), 1.0, 6.0, ((0, 32),), (0, 1, 32, 2.75))
    teacher = noise(streams_of[1], (TOKENS, D), 1.0, 6.0, ((0, 32),))
    valid_mask = with_ends((jax.random.randint(streams_of[2], (TOKENS,), 0, 4) < 3).astype(jnp.int32), jax.random.fold_in(streams_of[2], 1), 0, 1)
    doc_lengths = jax.vmap(lambda own: ragged_sizes(own, NDOC, SEQ_LEN, DOC_MOST, 2))(jax.random.split(streams_of[3], SEQS)).reshape((SEQS, NDOC)).astype(jnp.int32)
    gain_pre_attention = jnp.clip(1.0 + 0.18 * jax.random.normal(streams_of[4], (D,), jnp.float32), 0.099609375, 1.8984375).astype(jnp.bfloat16)
    query_weight = noise(streams_of[5], (D, HQ * HD), D ** -0.5, 0.125, ((0, 16), (1, 2)))
    key_weight = noise(streams_of[6], (D, KVH * HD), D ** -0.5, 0.125, ((0, 32),))
    value_weight = noise(streams_of[7], (D, KVH * HD), D ** -0.5, 0.125, ((0, 32),))
    output_weight = noise(streams_of[8], (HQ * HD, D), (HQ * HD) ** -0.5, 0.125, ((0, 2), (1, 16)))
    gain_post_attention = jnp.clip(1.0 + 0.18 * jax.random.normal(streams_of[9], (D,), jnp.float32), 0.099609375, 1.8984375).astype(jnp.bfloat16)
    gain_pre_feed = jnp.clip(1.0 + 0.18 * jax.random.normal(streams_of[10], (D,), jnp.float32), 0.099609375, 1.8984375).astype(jnp.bfloat16)
    gate_weight = noise(streams_of[11], (D, FF), D ** -0.5, 0.125, ((0, 16), (1, 2)))
    up_weight = noise(streams_of[12], (D, FF), D ** -0.5, 0.125, ((0, 16), (1, 2)))
    down_weight = noise(streams_of[13], (FF, D), FF ** -0.5, 0.0625, ((0, 2), (1, 16)))
    gain_post_feed = jnp.clip(1.0 + 0.18 * jax.random.normal(streams_of[14], (D,), jnp.float32), 0.099609375, 1.8984375).astype(jnp.bfloat16)
    return dict(inputs=inputs, teacher=teacher, valid_mask=valid_mask, doc_lengths=doc_lengths, gain_pre_attention=gain_pre_attention, query_weight=query_weight, key_weight=key_weight, value_weight=value_weight, output_weight=output_weight, gain_post_attention=gain_post_attention, gain_pre_feed=gain_pre_feed, gate_weight=gate_weight, up_weight=up_weight, down_weight=down_weight, gain_post_feed=gain_post_feed)


@jax.custom_vjp
def low(v):
    return lax.optimization_barrier(v.astype(jnp.bfloat16)).astype(jnp.float32)

@jax.custom_vjp
def low_back(v):
    return v

def low_keep(v):
    return (low(v), None)

def low_pass(kept, grad):
    return (grad,)

def back_keep(v):
    return (v, None)

def back_low(kept, grad):
    return (low(grad),)
low.defvjp(low_keep, low_pass)
low_back.defvjp(back_keep, back_low)
EPS = 1e-06
CAP = 50.0
SCALE = 0.0625
NEG = -1e+30
HIGH = lax.Precision.HIGHEST

def segment_ids(lengths, total_rows):
    ends_at = jnp.cumsum(lengths)
    places = jnp.arange(total_rows, dtype=jnp.int32)
    number = lax.optimization_barrier(jnp.sum((places[:, None] >= ends_at[None, :]).astype(jnp.int32), axis=1))
    return jnp.where(number == lengths.shape[0] - 1, -1, number).astype(jnp.int32)

def rms_scale(source, gain):
    return source * lax.rsqrt(lax.optimization_barrier(jnp.mean(source * source, axis=-1, keepdims=True)) + EPS) * gain

def attention(queries, keys_all, values_all, seg_all):
    seq_length = queries.shape[0]
    kv_total = keys_all.shape[1]
    group_size = HQ // kv_total
    query_rows = min(512, seq_length)
    places = jnp.arange(seq_length, dtype=jnp.int32)

    def one_block(number):
        first_row = number * query_rows
        rows_query = lax.dynamic_slice_in_dim(queries, first_row, query_rows).reshape(query_rows, kv_total, group_size, HD)
        rows_place = lax.dynamic_slice_in_dim(places, first_row, query_rows)
        rows_seg = lax.dynamic_slice_in_dim(seg_all, first_row, query_rows)
        raw_scores = low_back(jnp.einsum('qgjd,kgd->qgjk', rows_query, keys_all, precision=HIGH) * SCALE)
        capped = CAP * jnp.tanh(raw_scores / CAP)
        allowed = (places[None, :] <= rows_place[:, None]) & (seg_all[None, :] == rows_seg[:, None]) & ((seg_all[None, :] >= 0) | (places[None, :] == rows_place[:, None]))
        allowed = allowed[:, None, None, :]
        masked = jnp.where(allowed, capped, NEG)
        highest = lax.optimization_barrier(jnp.max(masked, axis=-1, keepdims=True))
        weights = jnp.where(allowed, jnp.exp(masked - highest), 0.0)
        probs = low(weights / lax.optimization_barrier(jnp.sum(weights, axis=-1, keepdims=True)))
        mixed = jnp.einsum('qgjk,kgd->qgjd', probs, values_all, precision=HIGH)
        return mixed.reshape(query_rows, HQ * HD)
    blocks_out = lax.map(jax.checkpoint(one_block), jnp.arange(seq_length // query_rows, dtype=jnp.int32))
    return blocks_out.reshape(seq_length, HQ * HD)

def layer(source, seg_all, params):
    gain_one, query_weight, key_weight, value_weight, output_weight, gain_two, gain_three, gate_weight, up_weight, down_weight, gain_four = params
    seq_length = source.shape[0]
    kv_total = max(KVH, N_SEQ)
    repeats = kv_total // KVH
    attention_in = low(rms_scale(source, gain_one))
    queries = low_back(low(jnp.dot(attention_in, query_weight, precision=HIGH))).reshape(seq_length, HQ, HD)
    keys_own = low_back(low(jnp.dot(attention_in, key_weight, precision=HIGH))).reshape(seq_length, KVH, HD)
    values_own = low_back(low(jnp.dot(attention_in, value_weight, precision=HIGH))).reshape(seq_length, KVH, HD)
    keys_all = low_back(jnp.repeat(keys_own, repeats, axis=1))
    values_all = low_back(jnp.repeat(values_own, repeats, axis=1))
    mixed = low_back(low(attention(queries, keys_all, values_all, seg_all)))
    branch_attention = low_back(jnp.dot(mixed, output_weight, precision=HIGH))
    hidden_state = source + rms_scale(branch_attention, gain_two)
    feed_in = low(rms_scale(hidden_state, gain_three))
    gate_value = low_back(jnp.dot(feed_in, gate_weight, precision=HIGH))
    up_value = low_back(jnp.dot(feed_in, up_weight, precision=HIGH))
    product_rows = low(jax.nn.gelu(gate_value, approximate=True) * up_value)
    branch_feed = low_back(jnp.dot(product_rows, down_weight, precision=HIGH))
    return hidden_state + rms_scale(branch_feed, gain_four)

def reference(inputs, teacher, valid_mask, doc_lengths, gain_pre_attention, query_weight, key_weight, value_weight, output_weight, gain_post_attention, gain_pre_feed, gate_weight, up_weight, down_weight, gain_post_feed):
    params = tuple((member.astype(jnp.float32) for member in (gain_pre_attention, query_weight, key_weight, value_weight, output_weight, gain_post_attention, gain_pre_feed, gate_weight, up_weight, down_weight, gain_post_feed)))
    seg_every = jax.vmap(lambda row_lengths: segment_ids(row_lengths, SEQ_LEN))(doc_lengths)
    live_every = ((valid_mask.reshape(SEQS, SEQ_LEN) == 1) & (seg_every >= 0)).reshape(TOKENS)
    count = jnp.maximum(jnp.sum(live_every.astype(jnp.float32)), 1.0)
    teacher_rows = teacher.astype(jnp.float32)
    source = inputs.astype(jnp.float32)
    layer_saved = jax.checkpoint(layer)

    def forward(source_rows, weights):

        def one_sequence(carry_value, pieces):
            return (carry_value, layer_saved(pieces[0], pieces[1], weights))
        carry_end, outputs = lax.scan(one_sequence, jnp.zeros((), jnp.float32), (source_rows.reshape(SEQS, SEQ_LEN, D), seg_every))
        layer_rows = outputs.reshape(TOKENS, D)
        difference = jnp.where(live_every[:, None], layer_rows - teacher_rows, 0.0)
        return (layer_rows, jnp.sum(difference * difference))
    (layer_rows, error_total), pullback = jax.vjp(forward, source, params)
    grad_source, gradients = pullback((jnp.zeros_like(layer_rows), TOKENS / count))
    loss_value = error_total / (D * count)
    return (layer_rows.astype(jnp.bfloat16), loss_value, grad_source, gradients[0], gradients[1], gradients[2], gradients[3], gradients[4], gradients[5], gradients[6], gradients[7], gradients[8], gradients[9], gradients[10])
```

```python
import jax
import jax.numpy as jnp
from jax import lax
from jax.sharding import PartitionSpec as P

HQ = 8
KVH = 4
HD = 256


EPS = 1e-06
CAP = 50.0
SCALE = 0.0625
NEG = -1e30


def segment_ids(lengths, total_rows):
    ends_at = jnp.cumsum(lengths)
    places = jnp.arange(total_rows, dtype=jnp.int32)
    number = jnp.sum((places[:, None] >= ends_at[None, :]).astype(jnp.int32), axis=1)
    return jnp.where(number == lengths.shape[0] - 1, -1, number)


def scale_rows(source, gain):
    inverse = lax.rsqrt(jnp.mean(source * source, axis=-1, keepdims=True) + EPS)
    return (source * inverse * gain, inverse)


def scale_back(source, inverse, gain, upstream):
    weighted = upstream * gain
    inner_mean = jnp.mean(weighted * source, axis=-1, keepdims=True)
    grad_source = inverse * weighted - source * (inverse * inverse * inverse) * inner_mean
    grad_gain = jnp.sum(upstream * source * inverse, axis=0)
    return (grad_source, grad_gain)


def inner_rows(left_side, right_side):
    return lax.dot_general(
        left_side, right_side, (((0,), (0,)), ((), ())), preferred_element_type=jnp.float32
    )


def against(left_side, right_side):
    return lax.dot_general(
        left_side, right_side, (((1,), (1,)), ((), ())), preferred_element_type=jnp.float32
    )


def geglu(gate_value, up_value):
    return jax.nn.gelu(gate_value, approximate=True) * up_value


def swap_pairs(size):
    return [(place, size - 1 - place) for place in range(size)]


def pair_gather(rows_here):
    if lax.axis_size("seq") != 2:
        return lax.all_gather(rows_here, "seq", axis=0, tiled=True)
    return jnp.concatenate([rows_here, lax.ppermute(rows_here, "seq", swap_pairs(2))], axis=0)


def pair_sum(partial):
    if lax.axis_size("seq") != 2:
        return lax.psum_scatter(
            partial.astype(jnp.bfloat16), "seq", scatter_dimension=0, tiled=True
        ).astype(jnp.float32)
    half = partial.shape[0] // 2
    arrived = lax.ppermute(partial[half:].astype(jnp.bfloat16), "seq", swap_pairs(2))
    return partial[:half] + arrived.astype(jnp.float32)


def pair_places(own_rows, seq_index, seq_size):
    if seq_size != 2:
        return jnp.arange(own_rows * seq_size, dtype=jnp.int32)
    here = jnp.arange(own_rows, dtype=jnp.int32)
    return jnp.concatenate([seq_index * own_rows + here, (1 - seq_index) * own_rows + here])


def seg_at(lengths, places):
    ends_at = jnp.cumsum(lengths)
    number = jnp.sum((places[:, None] >= ends_at[None, :]).astype(jnp.int32), axis=1)
    return jnp.where(number == lengths.shape[0] - 1, -1, number)


def columns_to_planes(matrix):
    planes = lax.axis_size("dp")
    rows, columns = matrix.shape
    return matrix.reshape(rows, planes, columns // planes).transpose(1, 0, 2)


def to_feed_order(rows_natural):
    planes, cycle = lax.axis_size("dp"), lax.axis_size("blk")
    rows, width = rows_natural.shape
    share = width // (planes * cycle)
    return (
        rows_natural.reshape(rows, planes, cycle, share).transpose(0, 2, 1, 3).reshape(rows, width)
    )


def from_feed_order(rows_feed):
    planes, cycle = lax.axis_size("dp"), lax.axis_size("blk")
    rows, width = rows_feed.shape
    share = width // (planes * cycle)
    return rows_feed.reshape(rows, cycle, planes, share).transpose(0, 2, 1, 3).reshape(rows, width)


def shards(
    inputs,
    teacher,
    valid_mask,
    doc_lengths,
    gain_pre_attention,
    query_weight,
    key_weight,
    value_weight,
    output_weight,
    gain_post_attention,
    gain_pre_feed,
    gate_weight,
    up_weight,
    down_weight,
    gain_post_feed,
):
    seq_size = lax.axis_size("seq")
    cycle_size = lax.axis_size("blk")
    planes = lax.axis_size("dp")
    own_rows = inputs.shape[0]
    width = inputs.shape[1]
    share = width // (planes * cycle_size)
    block_rows = own_rows * seq_size
    seq_length = block_rows * cycle_size
    heads_here = HQ // seq_size
    kv_total = max(KVH, seq_size)
    repeats = kv_total // KVH
    kv_here = kv_total // seq_size
    group_size = heads_here // kv_here
    cycle_index = lax.axis_index("blk")
    seq_index = lax.axis_index("seq")
    data_index = lax.axis_index("dp")
    seg_every = jax.vmap(lambda row_lengths: segment_ids(row_lengths, seq_length))(doc_lengths)
    live_every = ((valid_mask.reshape(seg_every.shape) == 1) & (seg_every >= 0)).reshape(-1)
    count = jnp.maximum(jnp.sum(live_every.astype(jnp.float32)), 1.0)
    token_total = float(seg_every.size)
    own_lengths = lax.dynamic_index_in_dim(doc_lengths, data_index, 0, keepdims=False)
    block_first = cycle_index * block_rows
    own_first = block_first + seq_index * own_rows
    live_own = lax.dynamic_slice_in_dim(live_every, data_index * seq_length + own_first, own_rows)
    in_block = pair_places(own_rows, seq_index, seq_size)
    positions = block_first + in_block
    key_places = (
        jnp.arange(cycle_size, dtype=jnp.int32)[:, None] * block_rows + in_block[None, :]
    ).reshape(-1)
    seg_block = seg_at(own_lengths, positions)
    seg_all = seg_at(own_lengths, key_places)

    gains = lax.all_gather(
        jnp.stack([gain_pre_attention, gain_post_attention, gain_pre_feed, gain_post_feed]),
        ("dp", "blk", "seq"),
        axis=0,
        tiled=False,
    )
    gains = gains.transpose(1, 0, 2).reshape(4, width).astype(jnp.float32)
    gain_first, gain_second, gain_third, gain_fourth = gains[0], gains[1], gains[2], gains[3]
    spread = max(1, seq_size // KVH)
    if seq_size <= KVH:
        kv_both = jnp.concatenate(
            [
                key_weight.reshape(-1, seq_size, KVH * HD // seq_size),
                value_weight.reshape(-1, seq_size, KVH * HD // seq_size),
            ],
            axis=2,
        ).transpose(1, 0, 2)
    else:
        kv_both = jnp.repeat(
            jnp.concatenate(
                [key_weight.reshape(-1, KVH, HD), value_weight.reshape(-1, KVH, HD)], axis=2
            ).transpose(1, 0, 2),
            spread,
            axis=0,
        )
    kv_mine = lax.all_to_all(kv_both, "seq", split_axis=0, concat_axis=0, tiled=True).reshape(
        share, 2 * kv_here * HD
    )
    project_local = jnp.concatenate([query_weight, kv_mine], axis=1)
    project_weight = lax.all_gather(project_local, ("dp", "blk"), axis=0, tiled=True)
    output_across = lax.all_gather(output_weight.T, ("dp", "blk"), axis=0, tiled=True)
    feed_local = jnp.concatenate(
        [
            columns_to_planes(gate_weight),
            columns_to_planes(up_weight),
            columns_to_planes(down_weight.T),
        ],
        axis=2,
    )
    feed_plane = lax.all_to_all(feed_local, "dp", split_axis=0, concat_axis=0, tiled=True)
    units = feed_plane.shape[2] // 3
    feed_weight = lax.all_gather(
        feed_plane.reshape(planes * share, 3 * units), "blk", axis=0, tiled=True
    )
    gate_matrix = feed_weight[:, :units]
    up_matrix = feed_weight[:, units : 2 * units]
    down_across = feed_weight[:, 2 * units :]

    source = inputs.astype(jnp.float32)
    normed_attention, inverse_one = scale_rows(source, gain_first)
    attention_in = normed_attention.astype(jnp.bfloat16)
    block_in = pair_gather(attention_in)
    projected = jnp.dot(block_in, project_weight, preferred_element_type=jnp.float32).astype(
        jnp.bfloat16
    )
    queries_group = projected[:, : heads_here * HD].reshape(block_rows, kv_here, group_size, HD)
    kv_block = projected[:, heads_here * HD :].reshape(block_rows, 2, kv_here, HD)
    kv_all = lax.all_gather(kv_block, "blk", axis=0, tiled=True)
    keys_all, values_all = kv_all[:, 0], kv_all[:, 1]

    raw_scores = (
        jnp.einsum("qgjd,kgd->gjqk", queries_group, keys_all, preferred_element_type=jnp.float32)
        * SCALE
    )
    capped = CAP * jnp.tanh(raw_scores / CAP)
    allowed = (
        (key_places[None, :] <= positions[:, None])
        & (seg_all[None, :] == seg_block[:, None])
        & ((seg_all[None, :] >= 0) | (key_places[None, :] == positions[:, None]))
    )[None, None]
    masked = jnp.where(allowed, capped, NEG)
    highest = jnp.max(masked, axis=-1, keepdims=True)
    weights = jnp.where(allowed, jnp.exp(masked - highest), 0.0)
    totals = jnp.sum(weights, axis=-1, keepdims=True)
    probs = (weights / totals).astype(jnp.bfloat16)
    log_totals = highest + jnp.log(totals)
    mixed = (
        jnp.einsum("gjqk,kgd->qgjd", probs, values_all, preferred_element_type=jnp.float32)
        .astype(jnp.bfloat16)
        .reshape(block_rows, heads_here * HD)
    )
    branch_attention = pair_sum(against(mixed, output_across))
    normed_branch, inverse_two = scale_rows(branch_attention, gain_second)
    hidden_state = source + normed_branch
    normed_feed, inverse_three = scale_rows(hidden_state, gain_third)
    feed_in = to_feed_order(normed_feed.astype(jnp.bfloat16))
    feed_rows = lax.all_gather(feed_in, ("dp", "seq"), axis=0, tiled=True)
    gate_value = jnp.dot(feed_rows, gate_matrix, preferred_element_type=jnp.float32)
    up_value = jnp.dot(feed_rows, up_matrix, preferred_element_type=jnp.float32)
    product_rows = geglu(gate_value, up_value).astype(jnp.bfloat16)
    branch_feed = from_feed_order(
        lax.psum_scatter(
            against(product_rows, down_across).astype(jnp.bfloat16),
            ("dp", "seq"),
            scatter_dimension=0,
            tiled=True,
        )
    ).astype(jnp.float32)
    normed_out, inverse_four = scale_rows(branch_feed, gain_fourth)
    layer_rows = hidden_state + normed_out
    difference = jnp.where(live_own[:, None], layer_rows - teacher.astype(jnp.float32), 0.0)
    error_own = jnp.sum(difference * difference)
    upstream = difference * (2.0 * token_total / count)

    grad_branch_feed, grad_gain_four = scale_back(branch_feed, inverse_four, gain_fourth, upstream)
    feed_grad_rows = lax.all_gather(
        to_feed_order(grad_branch_feed.astype(jnp.bfloat16)), ("dp", "seq"), axis=0, tiled=True
    )
    grad_product = jnp.dot(feed_grad_rows, down_across, preferred_element_type=jnp.float32)
    geglu_value, geglu_pull = jax.vjp(geglu, gate_value, up_value)
    grad_gate_value, grad_up_value = geglu_pull(grad_product)
    gate_back = grad_gate_value.astype(jnp.bfloat16)
    up_back = grad_up_value.astype(jnp.bfloat16)
    grad_feed_in = from_feed_order(
        lax.psum_scatter(
            (against(gate_back, gate_matrix) + against(up_back, up_matrix)).astype(jnp.bfloat16),
            ("dp", "seq"),
            scatter_dimension=0,
            tiled=True,
        )
    ).astype(jnp.float32)
    feed_grads = jnp.concatenate(
        [
            inner_rows(feed_rows, gate_back).astype(jnp.bfloat16),
            inner_rows(feed_rows, up_back).astype(jnp.bfloat16),
            inner_rows(feed_grad_rows, product_rows).astype(jnp.bfloat16),
        ],
        axis=1,
    )
    feed_plane_grads = lax.psum_scatter(feed_grads, "blk", scatter_dimension=0, tiled=True)
    feed_own_grads = lax.all_to_all(
        feed_plane_grads.reshape(planes, share, 3 * units),
        "dp",
        split_axis=0,
        concat_axis=0,
        tiled=True,
    ).astype(jnp.float32)

    def from_planes(part):
        return part.transpose(1, 0, 2).reshape(share, planes * units)

    gate_gradient = from_planes(feed_own_grads[:, :, :units])
    up_gradient = from_planes(feed_own_grads[:, :, units : 2 * units])
    down_gradient = from_planes(feed_own_grads[:, :, 2 * units :]).T

    grad_hidden_part, grad_gain_three = scale_back(
        hidden_state, inverse_three, gain_third, grad_feed_in
    )
    grad_hidden = upstream + grad_hidden_part
    grad_branch_attention, grad_gain_two = scale_back(
        branch_attention, inverse_two, gain_second, grad_hidden
    )
    branch_back = pair_gather(grad_branch_attention.astype(jnp.bfloat16))
    mixed_back = jnp.dot(branch_back, output_across, preferred_element_type=jnp.float32).astype(
        jnp.bfloat16
    )
    output_gradient = lax.psum_scatter(
        inner_rows(branch_back, mixed).astype(jnp.bfloat16),
        ("dp", "blk"),
        scatter_dimension=0,
        tiled=True,
    )
    mixed_group = mixed_back.reshape(block_rows, kv_here, group_size, HD)
    back_probs = jnp.where(allowed, jnp.exp(capped - log_totals), 0.0)
    grad_probs = jnp.einsum(
        "qgjd,kgd->gjqk", mixed_group, values_all, preferred_element_type=jnp.float32
    )
    centre = jnp.sum(back_probs * grad_probs, axis=-1, keepdims=True)
    score_back = (
        back_probs * (grad_probs - centre) * (1.0 - capped / CAP * (capped / CAP))
    ).astype(jnp.bfloat16)
    query_back = (
        (
            jnp.einsum("gjqk,kgd->qgjd", score_back, keys_all, preferred_element_type=jnp.float32)
            * SCALE
        )
        .astype(jnp.bfloat16)
        .reshape(block_rows, heads_here * HD)
    )
    grad_keys = (
        jnp.einsum("gjqk,qgjd->kgd", score_back, queries_group, preferred_element_type=jnp.float32)
        * SCALE
    )
    grad_values = jnp.einsum(
        "gjqk,qgjd->kgd",
        back_probs.astype(jnp.bfloat16),
        mixed_group,
        preferred_element_type=jnp.float32,
    )
    kv_back = lax.psum_scatter(
        jnp.stack([grad_keys, grad_values], axis=1).astype(jnp.bfloat16),
        "blk",
        scatter_dimension=0,
        tiled=True,
    ).reshape(block_rows, 2 * kv_here * HD)
    projected_back = jnp.concatenate([query_back, kv_back], axis=1)
    attention_back = pair_sum(against(projected_back, project_weight))
    project_gradient = lax.psum_scatter(
        inner_rows(block_in, projected_back).astype(jnp.bfloat16),
        ("dp", "blk"),
        scatter_dimension=0,
        tiled=True,
    )
    query_gradient = project_gradient[:, : heads_here * HD].astype(jnp.float32)
    kv_gradient = lax.all_to_all(
        project_gradient[:, heads_here * HD :].reshape(seq_size, share // seq_size, -1),
        "seq",
        split_axis=0,
        concat_axis=0,
        tiled=True,
    ).astype(jnp.float32)
    kv_gradient = jnp.sum(
        kv_gradient.reshape(
            seq_size // spread, spread, share // seq_size, 2, kv_total // seq_size * HD
        ),
        axis=1,
    ).transpose(2, 1, 0, 3).reshape(2, share // seq_size, KVH * HD)

    grad_source, grad_gain_one = scale_back(source, inverse_one, gain_first, attention_back)
    inputs_gradient = grad_hidden + grad_source
    pieces = jnp.concatenate(
        [
            jnp.stack([grad_gain_one, grad_gain_two, grad_gain_three, grad_gain_four]),
            jnp.full((4, 128), error_own, jnp.float32),
        ],
        axis=1,
    )
    summed = lax.psum(pieces, ("dp", "blk", "seq"))
    device_index = (data_index * cycle_size + cycle_index) * seq_size + seq_index
    gain_share = width // (planes * cycle_size * seq_size)
    gain_gradients = lax.dynamic_slice_in_dim(summed, device_index * gain_share, gain_share, axis=1)
    loss_value = summed[0, width] / (width * count)
    layer_output = layer_rows.astype(jnp.bfloat16)
    return (
        layer_output,
        loss_value,
        inputs_gradient,
        gain_gradients[0],
        query_gradient,
        kv_gradient[0],
        kv_gradient[1],
        output_gradient.astype(jnp.float32).T,
        gain_gradients[1],
        gain_gradients[2],
        gate_gradient,
        up_gradient,
        down_gradient,
        gain_gradients[3],
    )


def solution(mesh):
    in_specs = (
        P(("dp", "blk", "seq"), None),
        P(("dp", "blk", "seq"), None),
        P(),
        P(),
        P(("dp", "blk", "seq")),
        P(("dp", "blk"), "seq"),
        P(("dp", "blk", "seq"), None),
        P(("dp", "blk", "seq"), None),
        P("seq", ("dp", "blk")),
        P(("dp", "blk", "seq")),
        P(("dp", "blk", "seq")),
        P(("dp", "blk"), "seq"),
        P(("dp", "blk"), "seq"),
        P("seq", ("dp", "blk")),
        P(("dp", "blk", "seq")),
    )
    out_specs = (
        P(("dp", "blk", "seq"), None),
        P(),
        P(("dp", "blk", "seq"), None),
        P(("dp", "blk", "seq")),
        P(("dp", "blk"), "seq"),
        P(("dp", "blk", "seq"), None),
        P(("dp", "blk", "seq"), None),
        P("seq", ("dp", "blk")),
        P(("dp", "blk", "seq")),
        P(("dp", "blk", "seq")),
        P(("dp", "blk"), "seq"),
        P(("dp", "blk"), "seq"),
        P("seq", ("dp", "blk")),
        P(("dp", "blk", "seq")),
    )
    return jax.shard_map(shards, mesh=mesh, in_specs=in_specs, out_specs=out_specs, check_vma=False)
```
